512 devices in a mesh: blk: 32 (over x, z_lo), expert: 16 (over z_hi, y, core).
Axes of the slice: x: 4, y: 4, z: 16 (z_hi: 2, z_lo: 8; z = z_hi * 8 + z_lo), core: 2. Of those that a mesh axis runs over, the one named last changes fastest.
Arguments:
- short_draft: bfloat16 [1024, 64, 3, 512], P(('blk', 'expert')), may hold values from -42 to 42
- short_mask: int32 [1024, 64, 64], P(('blk', 'expert')), may hold values from 0 to 1, as said below
- short_keys: bfloat16 [1024, 128, 512], P(('blk', 'expert')), may hold values from -16 to 16
- short_values: bfloat16 [1024, 128, 512], P(('blk', 'expert')), may hold values from -6 to 6
- short_length: int32 [1024], P(('blk', 'expert')), may hold values from 1 to 128, 65536 in all
- short_x: bfloat16 [65536, 1024], P(('blk', 'expert')), may hold values from -44 to 44
- accepted: int32 [1024, 8], P(('blk', 'expert')), may hold values from 0 to 63, as said below
- long_draft: bfloat16 [32, 64, 3, 512], P('expert'), may hold values from -42 to 42
- long_mask: int32 [32, 64, 64], P('expert'), may hold values from 0 to 1, as said below
- long_keys: bfloat16 [32, 8192, 512], P('expert', 'blk'), may hold values from -15 to 15
- long_values: bfloat16 [32, 8192, 512], P('expert', 'blk'), may hold values from -6 to 6
- long_x: bfloat16 [32, 64, 1024], P('expert', 'blk'), may hold values from -44 to 44
- out_weight: bfloat16 [512, 1024], P('expert'), may hold values from -0.25 to 0.25
- norm_gain: bfloat16 [1024], replicated, may hold values from 0.099609375 to 1.8984375
- router: bfloat16 [1024, 16], replicated, may hold values from -0.1875 to 0.1875
- route_ids: int32 [67584, 2], P(('blk', 'expert')), may hold values from 0 to 15, all different within a row; in each aligned block of 132 rows (0 to 131, 132 to 263, ...) at most 21 rows name the same one
- expert_in: bfloat16 [16, 1408, 2, 1024], P('expert', 'blk'), may hold values from -0.1875 to 0.1875
- expert_out: bfloat16 [16, 1408, 1024], P('expert', 'blk'), may hold values from -0.15625 to 0.15625
Outputs:
- short_out: bfloat16 [65536, 1024], P(('blk', 'expert'))
- accepted_out: bfloat16 [1024, 8, 1024], P(('blk', 'expert'))
- long_out: bfloat16 [32, 64, 1024], P('expert', 'blk')
The draws below stay inside these ranges and needn't reach their ends.
Inputs may be any that keep to these rules, and one draw needn't show every extreme that they name: short_mask[r, i, j] is 1 exactly when tree node j is node i or one of its ancestors; every node but the root 0 has a parent of smaller index. long_mask[r, i, j] is 1 exactly when tree node j is node i or one of its ancestors; every node but the root 0 has a parent of smaller index. accepted[r] lists 8 nodes of request r's tree, the root first and node 63 last, each the parent of the next. `route_ids`: a row's two experts differ; among the rows of one device no expert is named more than 21 times.
All inputs are finite; a program needn't handle non-finite values. No bound on the sum of `short_length` on one device may be relied on, other than what follows from the above.
Results may differ from the reference program's by a relative error of at most 0.011.
Values may be sent and summed in bfloat16 or wider, within the bound.
A program may use at most 64 MiB of HBM per device.

```python
import math
import jax
import jax.numpy as jnp
import numpy as np
from jax import lax

D = 1024
HEADS = 8
HD = 64
FF = 1408
TREE = 64
ACC = 8
SHORT_LEN = 128
LONG_GRP = 2
SHORT_DEV = 2
LONG_DEV = 256
HW = 512
EXPERTS = 16
SHARE = 2
MOE_DEV = 132
CAP = 21
SREQ = 1024
LONG_REQ = 32
LONG_LEN = 8192
ROWS = 67584
N_BLK = 32
N_EXPERT = 16


def attach_last(parents):

    def climb(current, unused):
        return (parents[current], current)
    final_node, chain_nodes = lax.scan(climb, jnp.int32(TREE - 2), None, length=TREE)
    depth_count = jnp.sum((chain_nodes != 0).astype(jnp.int32))
    anchor = chain_nodes[depth_count - (ACC - 2)]
    return parents.at[TREE - 1].set(anchor.astype(jnp.int32))


def tree_parents(key, request_count):
    offsets = jax.random.randint(key, (request_count, TREE), 1, 5)
    node_ids = jnp.arange(TREE, dtype=jnp.int32)
    base_parents = jnp.maximum(node_ids[None, :] - offsets, 0).astype(jnp.int32)
    return jax.vmap(attach_last)(base_parents)


def ancestors(parents):
    node_ids = jnp.arange(TREE, dtype=jnp.int32)

    def add_node(current, ancestry):
        own_row = (node_ids == current).astype(jnp.int32)
        inherited = jnp.where(current > 0, ancestry[parents[current]], 0)
        return ancestry.at[current].set(jnp.maximum(own_row, inherited))
    return lax.fori_loop(0, TREE, add_node, jnp.zeros((TREE, TREE), jnp.int32))


def path_of(parents):

    def climb(current, unused):
        return (parents[current], current)
    final_node, chain_nodes = lax.scan(climb, jnp.int32(TREE - 1), None, length=TREE)
    depth_count = jnp.sum((chain_nodes != 0).astype(jnp.int32))
    positions = depth_count - jnp.arange(ACC, dtype=jnp.int32)
    return chain_nodes[positions]


def draft_projections(key, request_count):
    subkeys = jax.random.split(key, 3)
    array_shape = (request_count, TREE, HW)
    queries = jax.random.truncated_normal(subkeys[0], -6.0, 6.0, array_shape, jnp.float32)
    keyside = 7.0 * jax.random.truncated_normal(subkeys[1], -6.0, 6.0, array_shape, jnp.float32)
    values = jax.random.truncated_normal(subkeys[2], -6.0, 6.0, array_shape, jnp.float32)
    return jnp.stack([queries, keyside, values], axis=2).astype(jnp.bfloat16)


def stream_rows(key, array_shape):
    subkeys = jax.random.split(key, 3)
    noise_part = jax.random.truncated_normal(subkeys[0], -5.0, 5.0, array_shape, jnp.float32)
    columns = jax.random.uniform(subkeys[1], (array_shape[-1],), jnp.float32, math.log(0.3), math.log(3.0))
    row_scale = jax.random.uniform(subkeys[2], array_shape[:-1] + (1,), jnp.float32, math.log(0.5), math.log(2.0))
    return (noise_part * jnp.exp(columns) * jnp.exp(row_scale)).astype(jnp.bfloat16)


def draw_short_draft(key, part):
    return draft_projections(jax.random.fold_in(key, 22), SREQ)


def draw_long_draft(key, part):
    return draft_projections(jax.random.fold_in(key, 21), LONG_REQ)


def draw_short_mask(key, part):
    return jax.vmap(ancestors)(tree_parents(jax.random.fold_in(key, 11), SREQ))


def draw_accepted(key, part):
    return jax.vmap(path_of)(tree_parents(jax.random.fold_in(key, 11), SREQ))


def draw_long_mask(key, part):
    return jax.vmap(ancestors)(tree_parents(jax.random.fold_in(key, 12), LONG_REQ))


def draw_short_x(key, part):
    return stream_rows(jax.random.fold_in(key, 31), (SREQ * TREE, D))


def draw_long_x(key, part):
    return stream_rows(jax.random.fold_in(key, 32), (LONG_REQ, TREE, D))


def block_levels(stream_key, dims, cuts, smallest, largest):
    def one(dim, parts):
        steps = jax.random.uniform(jax.random.fold_in(jax.random.fold_in(stream_key, 6), dim), (parts,), jnp.float32, smallest / len(cuts), largest / len(cuts))
        return jnp.repeat(jnp.exp(steps), dims[dim] // parts).reshape((-1,) + (1,) * (len(dims) - dim - 1))

    factor_of = one(*cuts[0])
    for cut in cuts[1:]:
        factor_of = factor_of * one(*cut)
    return factor_of


def split_up(number_of, total, bound, skew):
    loads = [(1 << 20) // math.isqrt(rank ** skew) + 1 for rank in range(2, number_of + 1)]
    spare, given = total - bound - (number_of - 1), [1] * (number_of - 1)
    while spare > 0:
        candidates = [i for i in range(number_of - 1) if given[i] < bound]
        mass, budget = sum([loads[i] for i in candidates]), spare
        for i in candidates:
            extra = min(bound - given[i], max(1, budget * loads[i] // mass), spare)
            given[i] = given[i] + extra
            spare = spare - extra
    return np.array([bound] + given)


def ragged(own_key, amount, total, bound, lean):
    if amount == 2:
        one = jax.random.randint(own_key, (), max(1, total - bound), min(bound, total - 1) + 1)
        return jnp.stack([one, total - one])
    sizes = jnp.asarray(split_up(amount, total, bound, lean), jnp.int32)
    couples = (amount - 1) // 2
    donor, sink = sizes[1:1 + 2 * couples:2], sizes[2:2 + 2 * couples:2]
    margin = jnp.minimum(donor - 1, bound - sink)
    shifted = jax.random.randint(jax.random.fold_in(own_key, 1), (couples,), 0, 1 << 20) % (margin + 1)
    sizes = sizes.at[1:1 + 2 * couples:2].set(donor - shifted).at[2:2 + 2 * couples:2].set(sink + shifted)
    return sizes[jax.random.permutation(jax.random.fold_in(own_key, 2), amount)]


def shared_out(own_key, own, number, rows, amount, top, reach, skew):
    ranking = jax.random.permutation(own_key, amount)
    heavy_load, usual = shares(amount, rows * top, reach, skew, True), shares(amount, rows * top, reach, skew, False)
    places = jnp.arange(amount)

    def named(lengths, offset_by):
        used = int((lengths > 0).sum())
        fixed = max(1, used // 4)
        shifted = fixed + (places - fixed + offset_by * (used - fixed)) % max(1, amount - fixed)
        return jnp.zeros((amount,), jnp.int32).at[ranking[jnp.where(places < fixed, places, shifted)]].set(jnp.asarray(lengths, jnp.int32))

    lengths = jnp.where(number % 4 == 0, named(heavy_load, number // 4), named(usual, number - number // 4 - 1))
    mixed = jax.random.permutation(jax.random.fold_in(own, 3), amount)
    giver, taker = mixed[0:amount // 2 * 2:2], mixed[1:amount // 2 * 2:2]
    room = jnp.minimum(lengths[giver] - 1, reach - lengths[taker]) // 2
    room = jnp.where((giver == ranking[0]) | (taker == ranking[0]) | (lengths[taker] == 0), 0, jnp.maximum(room, 0))
    shifted = jax.random.randint(jax.random.fold_in(own, 4), (amount // 2,), 0, 1 << 20) % (room + 1)
    lengths = lengths.at[giver].add(-shifted).at[taker].add(shifted)
    items = jnp.searchsorted(jnp.cumsum(lengths), jnp.arange(rows * top), side="right").astype(jnp.int32)
    grid = items.reshape(top, rows).T
    grid = grid[jax.random.permutation(jax.random.fold_in(own, 1), rows)]
    offset_by = jax.random.randint(jax.random.fold_in(own, 2), (rows, 1), 0, top)
    return jnp.take_along_axis(grid, (jnp.arange(top)[None, :] + offset_by) % top, axis=1)


def shares(number_of, total, most, skew, full):
    loads = [(1 << 20) // math.isqrt(standing ** skew) + 1 for standing in range(1, number_of + 1)]
    largest = most if full else min(most, max(-(-total // number_of), total * loads[0] // sum(loads)))
    least = 1 if total - largest >= number_of - 1 else 0
    counts, surplus = [largest] + [least] * (number_of - 1), total - largest - least * (number_of - 1)
    while surplus > 0:
        free = [i for i in range(1, number_of) if counts[i] < largest] or [i for i in range(1, number_of) if counts[i] < most]
        mass, remaining = sum([loads[i] for i in free]), surplus
        for i in free:
            extra = min(most - counts[i], max(1, remaining * loads[i] // mass), surplus)
            counts[i] = counts[i] + extra
            surplus = surplus - extra
    return np.array(counts)


def noise(rng, extent, spread, bound, shards=(), held_as=jnp.bfloat16):
    values = spread * jax.random.normal(rng, extent, jnp.float32)
    if shards:
        values = values * block_levels(rng, extent, shards, -0.22, 0.18)
    return jnp.clip(values, -bound, bound).astype(held_as)


def setup_inputs(seed: int = 0) -> dict:
    splits = jax.random.split(jax.random.key(seed), 19)
    short_draft = draw_short_draft(jax.random.fold_in(splits[18], 71), 0)
    short_mask = draw_short_mask(jax.random.fold_in(splits[18], 71), 0)
    short_keys = noise(splits[2], (SREQ, SHORT_LEN, HW), 4.0, 16.0, ((0, 512),))
    short_values = noise(splits[3], (SREQ, SHORT_LEN, HW), 1.0, 6.0, ((0, 512),))
    short_length = ragged(splits[4], SREQ, SREQ * SHORT_LEN // 2, SHORT_LEN, 0).astype(jnp.int32)
    short_x = draw_short_x(jax.random.fold_in(splits[18], 71), 0)
    accepted = draw_accepted(jax.random.fold_in(splits[18], 71), 0)
    long_draft = draw_long_draft(jax.random.fold_in(splits[18], 71), 0)
    long_mask = draw_long_mask(jax.random.fold_in(splits[18], 71), 0)
    long_keys = noise(splits[9], (LONG_REQ, LONG_LEN, HW), 2.5, 15.0, ((0, 16), (1, 32)))
    long_values = noise(splits[10], (LONG_REQ, LONG_LEN, HW), 1.0, 6.0, ((0, 16), (1, 32)))
    long_x = draw_long_x(jax.random.fold_in(splits[18], 71), 0)
    out_weight = noise(splits[12], (HW, D), HW ** -0.5, 0.25, ((0, 16),))
    norm_gain = jnp.clip(1.0 + 0.18 * jax.random.normal(splits[13], (D,), jnp.float32), 0.099609375, 1.8984375).astype(jnp.bfloat16)
    router = noise(splits[14], (D, EXPERTS), D ** -0.5, 0.1875)
    route_ids_keys = jax.random.split(jax.random.fold_in(splits[15], 1), ROWS // MOE_DEV)
    route_ids_turns = jax.random.permutation(jax.random.fold_in(splits[15], 3), ROWS // MOE_DEV)
    route_ids = jax.vmap(lambda own, number: shared_out(jax.random.fold_in(splits[15], 2), own, number, MOE_DEV, EXPERTS, 2, CAP, 2))(route_ids_keys, route_ids_turns).reshape((ROWS, 2))
    expert_in = noise(splits[16], (EXPERTS, FF, 2, D), D ** -0.5, 0.1875, ((0, 16), (1, 32)))
    expert_out = noise(splits[17], (EXPERTS, FF, D), FF ** -0.5, 0.15625, ((0, 16), (1, 32)))
    return dict(short_draft=short_draft, short_mask=short_mask, short_keys=short_keys, short_values=short_values, short_length=short_length, short_x=short_x, accepted=accepted, long_draft=long_draft, long_mask=long_mask, long_keys=long_keys, long_values=long_values, long_x=long_x, out_weight=out_weight, norm_gain=norm_gain, router=router, route_ids=route_ids, expert_in=expert_in, expert_out=expert_out)


def round_trip(tensor):
    return lax.optimization_barrier(tensor.astype(jnp.bfloat16)).astype(jnp.float32)

def block_part(queries, keyside, values, allowed):
    scores = jnp.einsum('qhe,khe->qhk', queries, keyside) * HD ** (-0.5)
    scores = jnp.where(allowed[:, None, :], scores, -jnp.inf)
    peaks = lax.optimization_barrier(jnp.max(scores, axis=-1))
    weights = round_trip(jnp.exp(scores - peaks[..., None]))
    totals = lax.optimization_barrier(jnp.sum(weights, axis=-1))
    output = jnp.einsum('qhk,khe->qhe', weights, values)
    return (peaks, totals, output)

def join_blocks(peaks, totals, output):
    highest = lax.optimization_barrier(jnp.max(peaks, axis=0))
    factor = jnp.exp(peaks - highest)
    denominator = lax.optimization_barrier(jnp.sum(factor * totals, axis=0))
    numerator = lax.optimization_barrier(jnp.sum(factor[..., None] * output, axis=0))
    joined = numerator / denominator[..., None]
    return joined.reshape(joined.shape[0], HW).astype(jnp.bfloat16)

def split_draft(draft_rows):
    wide = draft_rows.astype(jnp.float32).reshape(TREE, 3, HEADS, HD)
    return (wide[:, 0], wide[:, 1], wide[:, 2])

def short_attend(packed):
    draft_rows, cache_keys, cache_values, length, tree_mask = packed
    queries, tree_keys, tree_values = split_draft(draft_rows)
    cache_k = cache_keys.astype(jnp.float32).reshape(SHORT_LEN, HEADS, HD)
    cache_v = cache_values.astype(jnp.float32).reshape(SHORT_LEN, HEADS, HD)
    visible = jnp.broadcast_to(jnp.arange(SHORT_LEN)[None, :] < length, (TREE, SHORT_LEN))
    cache_part = block_part(queries, cache_k, cache_v, visible)
    tree_part = block_part(queries, tree_keys, tree_values, tree_mask == 1)
    stacked = tuple((jnp.stack([former, latter]) for former, latter in zip(cache_part, tree_part)))
    return join_blocks(*stacked)

def long_attend(packed):
    draft_rows, cache_keys, cache_values, tree_mask = packed
    queries, tree_keys, tree_values = split_draft(draft_rows)
    cache_k = cache_keys.astype(jnp.float32).reshape(N_BLK, LONG_DEV, HEADS, HD)
    cache_v = cache_values.astype(jnp.float32).reshape(N_BLK, LONG_DEV, HEADS, HD)
    everything = jnp.ones((TREE, LONG_DEV), dtype=bool)
    cache_parts = jax.vmap(block_part, in_axes=(None, 0, 0, None))(queries, cache_k, cache_v, everything)
    tree_part = block_part(queries, tree_keys, tree_values, tree_mask == 1)
    stacked = tuple((jnp.concatenate([blockwise, single[None]], axis=0) for blockwise, single in zip(cache_parts, tree_part)))
    return join_blocks(*stacked)

def reference(short_draft, short_mask, short_keys, short_values, short_length, short_x, accepted, long_draft, long_mask, long_keys, long_values, long_x, out_weight, norm_gain, router, route_ids, expert_in, expert_out):
    short_attn = lax.map(short_attend, (short_draft, short_keys, short_values, short_length, short_mask))
    long_attn = lax.map(long_attend, (long_draft, long_keys, long_values, long_mask))
    short_state = (short_x.astype(jnp.float32) + jnp.dot(short_attn.reshape(SREQ * TREE, HW), out_weight, preferred_element_type=jnp.float32)).astype(jnp.bfloat16)
    long_state = (long_x.reshape(LONG_REQ * TREE, D).astype(jnp.float32) + jnp.dot(long_attn.reshape(LONG_REQ * TREE, HW), out_weight, preferred_element_type=jnp.float32)).astype(jnp.bfloat16)
    device_count = N_BLK * N_EXPERT
    short_rows = short_state.reshape(device_count, SHORT_DEV * TREE, D)
    long_rows = long_state.reshape(N_EXPERT, LONG_GRP, N_BLK, SHARE, D).transpose(2, 0, 1, 3, 4).reshape(device_count, LONG_GRP * SHARE, D)
    layer_state = jnp.concatenate([short_rows, long_rows], axis=1).reshape(ROWS, D)
    state_wide = layer_state.astype(jnp.float32)
    normed = (state_wide * lax.rsqrt(lax.optimization_barrier(jnp.mean(state_wide * state_wide, axis=-1, keepdims=True)) + 1e-06) * norm_gain.astype(jnp.float32)).astype(jnp.bfloat16)
    gate_probs = jax.nn.sigmoid(jnp.dot(normed, router, preferred_element_type=jnp.float32))

    def expert_pass(moe_total, packed):
        weight_in, weight_out, expert = packed
        chosen = jnp.any(route_ids == expert, axis=1)
        picked = jnp.nonzero(chosen, size=device_count * CAP, fill_value=0)[0].astype(jnp.int32)
        is_valid = jnp.arange(device_count * CAP) < jnp.sum(chosen.astype(jnp.int32))
        inputs = normed[picked]
        gate_part = jnp.dot(inputs, weight_in[:, 0, :].T, preferred_element_type=jnp.float32)
        up_part = jnp.dot(inputs, weight_in[:, 1, :].T, preferred_element_type=jnp.float32)
        inner_act = (jax.nn.gelu(gate_part, approximate=True) * up_part).astype(jnp.bfloat16)
        result = round_trip(jnp.dot(inner_act, weight_out, preferred_element_type=jnp.float32))
        row_gate = jnp.where(is_valid, gate_probs[picked, expert], 0.0)
        return (moe_total.at[picked].add(row_gate[:, None] * result), None)
    moe_total, unused = lax.scan(expert_pass, jnp.zeros((ROWS, D), jnp.float32), (expert_in, expert_out, jnp.arange(EXPERTS, dtype=jnp.int32)))
    layer_out = (state_wide + moe_total).astype(jnp.bfloat16).reshape(device_count, MOE_DEV, D)
    short_out = layer_out[:, :SHORT_DEV * TREE].reshape(SREQ * TREE, D)
    long_out = layer_out[:, SHORT_DEV * TREE:].reshape(N_BLK, N_EXPERT, LONG_GRP, SHARE, D).transpose(1, 2, 0, 3, 4).reshape(LONG_REQ, TREE, D)
    accepted_out = jnp.take_along_axis(short_out.reshape(SREQ, TREE, D), accepted[:, :, None].astype(jnp.int32), axis=1)
    return (short_out, accepted_out, long_out)
```

```python
import jax
import jax.numpy as jnp
from jax import lax
from jax.sharding import PartitionSpec as P

HEADS = 8
HD = 64


def xor_exchange(array, axis, size, bit):
    return lax.ppermute(array, axis, [(i, i ^ bit) for i in range(size)])


def shift_x(array, step):
    pairs = [(i, ((i // 8 + step) % 4) * 8 + i % 8) for i in range(32)]
    return lax.ppermute(array, "blk", pairs)


def gather_blk(block):
    for bit in (2, 1):
        block = jnp.concatenate([block, xor_exchange(block, "blk", 32, bit)], axis=0)
    half = block.shape[0] // 2
    before = shift_x(block, 1)
    after = shift_x(block, -1)
    far = (shift_x(before[:half], 1), shift_x(after[half:], -1))
    return (block, before, after) + far


def gather_expert(block):
    rows, columns = block.shape
    place = lax.axis_index("expert")
    for axis, bit in enumerate((8, 4, 2, 1)):
        other = xor_exchange(block, "expert", 16, bit)
        mine_first = (place // bit) % 2 == 0
        first = jnp.where(mine_first, block, other)
        second = jnp.where(mine_first, other, block)
        block = jnp.stack([first, second], axis=axis)
    return block.reshape(16 * rows, columns)


def scatter_parts(part, share_rows, blocks):
    peaks, totals, output = part
    count, tree = peaks.shape[:2]
    packed = jnp.concatenate([output, peaks, totals], axis=-1)
    width = packed.shape[-1]
    packed = packed.reshape(count, tree // share_rows, share_rows, width).transpose(1, 0, 2, 3)
    arrived = lax.all_to_all(packed, "blk", split_axis=0, concat_axis=0, tiled=True)
    others = [xor_exchange(block, "blk", 32, 4) for block in blocks]
    arrived, others = lax.optimization_barrier((arrived, others))
    pairs = [jnp.concatenate(pair, axis=0) for pair in zip(blocks, others)]
    wide = output.shape[-1]
    part = (
        arrived[..., wide : wide + HEADS],
        arrived[..., wide + HEADS :],
        arrived[..., :wide],
    )
    return part, pairs


def join_many(parts):
    peaks, totals, output = parts
    highest = jnp.max(peaks, axis=0)
    scale = jnp.exp(peaks - highest[None])
    return (
        highest,
        jnp.sum(scale * totals, axis=0),
        jnp.sum(expand(scale, output), axis=0),
    )


def heads_of(tensor):
    return tensor.reshape(tensor.shape[:-1] + (HEADS, HD))


def block_part(queries, keyside, values, allowed):
    head_size = queries.shape[-1]
    scores = jnp.einsum(
        "rqhe,rkhe->rqhk", queries, keyside, preferred_element_type=jnp.float32
    ) * head_size ** (-0.5)
    scores = jnp.where(allowed[:, :, None, :], scores, -jnp.inf)
    peaks = jnp.max(scores, axis=-1)
    weights = jnp.exp(scores - peaks[..., None]).astype(jnp.bfloat16)
    totals = jnp.sum(weights.astype(jnp.float32), axis=-1)
    output = jnp.einsum("rqhk,rkhe->rqhe", weights, values, preferred_element_type=jnp.float32)
    return (peaks, totals, output.reshape(output.shape[0], output.shape[1], -1))


def expand(factor, output):
    shaped = output.reshape(factor.shape + (-1,))
    return (shaped * factor[..., None]).reshape(output.shape)


def divide(output, totals):
    shaped = output.reshape(totals.shape + (-1,))
    return (shaped / totals[..., None]).reshape(output.shape)


def pair_join(former, latter):
    highest = jnp.maximum(former[0], latter[0])
    former_scale = jnp.exp(former[0] - highest)
    latter_scale = jnp.exp(latter[0] - highest)
    totals = former_scale * former[1] + latter_scale * latter[1]
    output = expand(former_scale, former[2]) + expand(latter_scale, latter[2])
    return (highest, totals, output)


def finish(joined):
    return divide(joined[2], joined[1]).astype(jnp.bfloat16)


def on_device(
    short_draft,
    short_mask,
    short_keys,
    short_values,
    short_length,
    short_x,
    accepted,
    long_draft,
    long_mask,
    long_keys,
    long_values,
    long_x,
    out_weight,
    norm_gain,
    router,
    route_ids,
    expert_in,
    expert_out,
):
    short_count = short_draft.shape[0]
    tree_size = short_draft.shape[1]
    cache_size = short_keys.shape[1]
    model_width = out_weight.shape[1]
    short_queries = heads_of(short_draft[:, :, 0])
    visible = jnp.broadcast_to(
        jnp.arange(cache_size)[None, None, :] < short_length[:, None, None],
        (short_count, tree_size, cache_size),
    )
    short_cache = block_part(short_queries, heads_of(short_keys), heads_of(short_values), visible)
    short_tree = block_part(
        short_queries,
        heads_of(short_draft[:, :, 1]),
        heads_of(short_draft[:, :, 2]),
        short_mask == 1,
    )
    short_attn = finish(pair_join(short_cache, short_tree))
    long_count = long_keys.shape[0]
    cache_local = long_keys.shape[1]
    long_queries = heads_of(long_draft[:, :, 0])
    everything = jnp.ones((long_count, tree_size, cache_local), dtype=bool)
    local_part = block_part(long_queries, heads_of(long_keys), heads_of(long_values), everything)
    share_rows = tree_size // lax.axis_size("blk")
    share_start = lax.axis_index("blk") * share_rows
    arrived, weights = scatter_parts(
        local_part, share_rows, (expert_in[0, :, 0, :], expert_in[0, :, 1, :], expert_out[0])
    )
    cache_part = join_many(arrived)
    share_queries = lax.dynamic_slice_in_dim(long_queries, share_start, share_rows, 1)
    share_mask = lax.dynamic_slice_in_dim(long_mask, share_start, share_rows, 1)
    long_tree = block_part(
        share_queries, heads_of(long_draft[:, :, 1]), heads_of(long_draft[:, :, 2]), share_mask == 1
    )
    long_attn = finish(pair_join(cache_part, long_tree))
    attn_rows = jnp.concatenate(
        [short_attn.reshape(-1, short_attn.shape[-1]), long_attn.reshape(-1, long_attn.shape[-1])],
        axis=0,
    )
    residual = jnp.concatenate([short_x, long_x.reshape(-1, model_width)], axis=0)
    row_count = attn_rows.shape[0]
    projected = jnp.dot(
        attn_rows,
        gather_expert(out_weight),
        preferred_element_type=jnp.float32,
    )
    layer_state = (residual.astype(jnp.float32) + projected).astype(jnp.bfloat16)
    state_wide = layer_state.astype(jnp.float32)
    normed = (
        state_wide
        * lax.rsqrt(jnp.mean(state_wide * state_wide, axis=-1, keepdims=True) + 1e-06)
        * norm_gain.astype(jnp.float32)
    ).astype(jnp.bfloat16)
    gate_probs = jax.nn.sigmoid(jnp.dot(normed, router, preferred_element_type=jnp.float32))
    expert_count = router.shape[1]
    capacity = (row_count * 10 + 4 * expert_count - 1) // (4 * expert_count)
    one_hot = route_ids[:, :, None] == jnp.arange(expert_count, dtype=jnp.int32)[None, None, :]
    gate_pick = jnp.sum(jnp.where(one_hot, gate_probs[:, None, :], 0.0), axis=-1)
    flat_hot = one_hot.reshape(2 * row_count, expert_count).astype(jnp.int32)
    earlier = jnp.cumsum(flat_hot, axis=0) - flat_hot
    slot_in = jnp.sum(earlier * flat_hot, axis=-1)
    target = route_ids.reshape(-1) * capacity + slot_in
    placement = (
        jnp.arange(expert_count * capacity, dtype=jnp.int32)[:, None] == target[None, :]
    ).astype(jnp.bfloat16)
    dispatch = jnp.dot(
        placement, jnp.repeat(normed, 2, axis=0), preferred_element_type=jnp.float32
    ).astype(jnp.bfloat16)
    dispatch = dispatch.reshape(expert_count, capacity, model_width)
    received = lax.all_to_all(dispatch, "expert", split_axis=0, concat_axis=0, tiled=True)
    flat_rows = received.reshape(-1, model_width)
    gate_blocks, up_blocks, out_blocks = [gather_blk(block) for block in weights]
    expert_sum = jnp.zeros((flat_rows.shape[0], model_width), jnp.float32)
    for gate_block, up_block, out_block in zip(gate_blocks, up_blocks, out_blocks):
        gate_part = jnp.einsum(
            "rd,nd->rn", flat_rows, gate_block, preferred_element_type=jnp.float32
        )
        up_part = jnp.einsum(
            "rd,nd->rn", flat_rows, up_block, preferred_element_type=jnp.float32
        )
        inner_act = (jax.nn.gelu(gate_part, approximate=True) * up_part).astype(jnp.bfloat16)
        expert_sum = expert_sum + jnp.dot(
            inner_act, out_block, preferred_element_type=jnp.float32
        )
    expert_y = expert_sum.astype(jnp.bfloat16).reshape(expert_count, capacity, model_width)
    returned = lax.all_to_all(expert_y, "expert", split_axis=0, concat_axis=0, tiled=True)
    per_route = jnp.einsum(
        "sa,sd->ad",
        placement,
        returned.reshape(-1, model_width),
        preferred_element_type=jnp.float32,
    )
    moe_sum = jnp.sum(per_route.reshape(row_count, 2, model_width) * gate_pick[:, :, None], axis=1)
    layer_out = (state_wide + moe_sum).astype(jnp.bfloat16)
    short_total = short_x.shape[0]
    short_out = layer_out[:short_total]
    long_out = layer_out[short_total:].reshape(long_x.shape)
    accepted_out = jnp.take_along_axis(
        short_out.reshape(short_count, tree_size, model_width), accepted[:, :, None], axis=1
    )
    return (short_out, accepted_out, long_out)


def solution(mesh):
    return jax.shard_map(
        on_device,
        mesh=mesh,
        in_specs=(
            P(("blk", "expert"), None, None, None),
            P(("blk", "expert"), None, None),
            P(("blk", "expert"), None, None),
            P(("blk", "expert"), None, None),
            P(("blk", "expert")),
            P(("blk", "expert"), None),
            P(("blk", "expert"), None),
            P("expert", None, None, None),
            P("expert", None, None),
            P("expert", "blk", None),
            P("expert", "blk", None),
            P("expert", "blk", None),
            P("expert", None),
            P(),
            P(),
            P(("blk", "expert"), None),
            P("expert", "blk", None, None),
            P("expert", "blk", None),
        ),
        out_specs=(
            P(("blk", "expert"), None),
            P(("blk", "expert"), None, None),
            P("expert", "blk", None),
        ),
        check_vma=False,
    )
```

```python
import functools

import jax
import jax.numpy as jnp
from jax import lax
from jax.experimental import pallas as pl
from jax.experimental.pallas import tpu as pltpu
from jax.sharding import PartitionSpec as P

HEADS = 8
HD = 64


LINE = 8
RING = 4
SLOT = 48


def sends_of(condition, descriptor, started):
    @pl.when(condition)
    def _():
        descriptor().start()

    started.append((condition, descriptor))


def remote(source, target, send_sem, recv_sem, device):
    return pltpu.make_async_remote_copy(
        src_ref=source,
        dst_ref=target,
        send_sem=send_sem,
        recv_sem=recv_sem,
        device_id=device,
        device_id_type=pl.DeviceIdType.MESH,
    )


def signal(barrier, device):
    pl.semaphore_signal(barrier, inc=1, device_id=device, device_id_type=pl.DeviceIdType.MESH)


def gather_kernel(count, with_rows, *refs):
    inputs = refs[:count]
    refs = refs[count:]
    if with_rows:
        rows_in, refs = refs[0], refs[1:]
    outputs = refs[:count]
    refs = refs[count:]
    if with_rows:
        rows_out, refs = refs[0], refs[1:]
    local_sem, recv_sem, up_sem, down_sem, right_sem, left_sem, far_sem = refs[:7]
    if with_rows:
        rows_local, rows_recv, rows_send = refs[7:]
    blk = lax.axis_index("blk")
    x = blk // LINE
    z = blk % LINE
    right = {"blk": ((x + 1) % RING) * LINE + z}
    left = {"blk": ((x + RING - 1) % RING) * LINE + z}
    above = {"blk": blk + 1}
    below = {"blk": blk - 1}
    has_up = z < LINE - 1
    has_down = z > 0
    started = []

    barrier = pltpu.get_barrier_semaphore()
    signal(barrier, right)
    signal(barrier, left)

    @pl.when(has_up)
    def _():
        signal(barrier, above)

    @pl.when(has_down)
    def _():
        signal(barrier, below)

    neighbours = 2 + has_up.astype(jnp.int32) + has_down.astype(jnp.int32)
    if with_rows:
        place = lax.axis_index("expert")
        half = place // 8
        y = (place // 2) % 4
        core = place % 2

        def at(h, row, c):
            return (h % 2) * 8 + (row % 4) * 2 + c % 2

        across = {"expert": at(half + 1, y, core)}
        partner = {"expert": at(half, y, core + 1)}
        ahead = {"expert": at(half, y + 1, core)}
        behind = {"expert": at(half, y + 3, core)}
        for device in (across, partner, ahead, behind):
            signal(barrier, device)
        neighbours = neighbours + 4
    pl.semaphore_wait(barrier, neighbours)

    def send(k, slot, source, sem, device):
        return lambda: remote(source(), outputs[k].at[slot], sem, recv_sem.at[k, slot], device)

    def arrive(k, slot):
        piece = outputs[k].at[slot]
        remote(piece, piece, far_sem.at[k, 0], recv_sem.at[k, slot], right).wait_recv()

    def row_send(index, slot, source, device):
        copy = remote(source, rows_out.at[slot], rows_send.at[index], rows_recv.at[slot], device)
        copy.start()
        row_started.append(copy)

    def row_arrive(slot):
        piece = rows_out.at[slot]
        remote(piece, piece, rows_send.at[0], rows_recv.at[slot], across).wait_recv()

    row_started = []
    always = z >= 0
    if with_rows:
        row_send(0, place, rows_in, across)
        own_rows = pltpu.make_async_copy(rows_in, rows_out.at[place], rows_local)
        own_rows.start()

    own_copies = []
    for k in range(count):
        own = lambda k=k: inputs[k]
        sends_of(has_up, send(k, blk, own, up_sem.at[k, 0], above), started)
        sends_of(has_down, send(k, blk, own, down_sem.at[k, 0], below), started)
        sends_of(always, send(k, blk, own, right_sem.at[k, 0], right), started)
        sends_of(always, send(k, blk, own, left_sem.at[k, 0], left), started)
        copy = pltpu.make_async_copy(inputs[k], outputs[k].at[blk], local_sem.at[k])
        copy.start()
        own_copies.append(copy)

    for distance in range(1, LINE):
        for direction in (0, 1):
            slot = blk - distance if direction == 0 else blk + distance
            present = z >= distance if direction == 0 else z + distance < LINE
            onward = has_up if direction == 0 else has_down
            target = above if direction == 0 else below
            z_sem = up_sem if direction == 0 else down_sem
            index = distance + direction * LINE
            for k in range(count):
                held = lambda k=k, slot=slot: outputs[k].at[slot]

                @pl.when(present)
                def _(k=k, slot=slot):
                    arrive(k, slot)

                sends_of(
                    jnp.logical_and(present, onward),
                    send(k, slot, held, z_sem.at[k, distance], target),
                    started,
                )
                sends_of(present, send(k, slot, held, right_sem.at[k, index], right), started)
                sends_of(present, send(k, slot, held, left_sem.at[k, index], left), started)
        if with_rows and distance == 2:
            row_arrive(at(half + 1, y, core))
            for h in range(2):
                slot = at(half + h, y, core)
                source = rows_in if h == 0 else rows_out.at[slot]
                row_send(1 + h, slot, source, partner)
        if with_rows and distance == 3:
            for h in range(2):
                row_arrive(at(half + h, y, core + 1))
            for h in range(2):
                for c in range(2):
                    slot = at(half + h, y, core + c)
                    source = rows_in if h + c == 0 else rows_out.at[slot]
                    row_send(3 + 2 * h + c, slot, source, ahead)
                    row_send(7 + 2 * h + c, slot, source, behind)
        if with_rows and distance == 6:
            for c in range(2):
                for h in range(2):
                    row_arrive(at(h, y + 3, c))
                    row_arrive(at(h, y + 1, c))
                slot = at(0, y + 3, c)
                row_send(11 + c, slot, rows_out.at[slot], ahead)
                slot = at(1, y + 1, c)
                row_send(13 + c, slot, rows_out.at[slot], behind)

    before = ((x + RING - 1) % RING) * LINE
    after = ((x + 1) % RING) * LINE
    opposite = ((x + 2) % RING) * LINE
    for order in range(LINE):
        for k in range(count):
            line = (z + order) % LINE
            from_left, from_right = before + line, after + line
            arrive(k, from_left)
            arrive(k, from_right)
            sem = far_sem.at[k, order]
            even = line % 2 == 0
            first = lambda k=k, slot=from_left: outputs[k].at[slot]
            second = lambda k=k, slot=from_right: outputs[k].at[slot]
            sends_of(even, send(k, from_left, first, sem, right), started)
            sends_of(jnp.logical_not(even), send(k, from_right, second, sem, left), started)
    for line in range(LINE):
        for k in range(count):
            arrive(k, opposite + line)
    if with_rows:
        for h in range(2):
            for c in range(2):
                row_arrive(at(h, y + 2, c))
        for copy in row_started:
            copy.wait_send()
        own_rows.wait()
    for copy in own_copies:
        copy.wait()
    for condition, descriptor in started:

        @pl.when(condition)
        def _(descriptor=descriptor):
            descriptor().wait_send()


def gather_blocks(blocks, rows, collective_id):
    count = len(blocks)
    with_rows = rows is not None
    blocks = [jnp.pad(block, ((0, SLOT - block.shape[0]), (0, 0))) for block in blocks]
    width = blocks[0].shape[1]
    dma = pltpu.SemaphoreType.DMA
    shapes = [jax.ShapeDtypeStruct((RING * LINE, SLOT, width), jnp.bfloat16)] * count
    operands = list(blocks)
    scratch = [
        dma((count,)),
        dma((count, RING * LINE)),
        dma((count, LINE)),
        dma((count, LINE)),
        dma((count, 2 * LINE)),
        dma((count, 2 * LINE)),
        dma((count, LINE)),
    ]
    if with_rows:
        operands.append(rows)
        shapes.append(jax.ShapeDtypeStruct((16,) + rows.shape, jnp.bfloat16))
        scratch += [dma(()), dma((16,)), dma((15,))]
    gathered = pl.pallas_call(
        functools.partial(gather_kernel, count, with_rows),
        out_shape=shapes,
        in_specs=[pl.BlockSpec(memory_space=pltpu.VMEM)] * len(operands),
        out_specs=[pl.BlockSpec(memory_space=pl.ANY)] * len(shapes),
        scratch_shapes=scratch,
        compiler_params=pltpu.CompilerParams(collective_id=collective_id, has_side_effects=True),
        cost_estimate=pl.CostEstimate(
            flops=0, bytes_accessed=100_000_000 * count, transcendentals=0
        ),
    )(*operands)
    return [array.reshape(-1, array.shape[-1]) for array in gathered]


def scatter_parts(part, share_rows):
    peaks, totals, output = part
    count, tree = peaks.shape[:2]
    packed = jnp.concatenate([output, peaks, totals], axis=-1)
    width = packed.shape[-1]
    packed = packed.reshape(count, tree // share_rows, share_rows, width).transpose(1, 0, 2, 3)
    arrived = lax.all_to_all(packed, "blk", split_axis=0, concat_axis=0, tiled=True)
    wide = output.shape[-1]
    return (
        arrived[..., wide : wide + HEADS],
        arrived[..., wide + HEADS :],
        arrived[..., :wide],
    )


def join_many(parts):
    peaks, totals, output = parts
    highest = jnp.max(peaks, axis=0)
    scale = jnp.exp(peaks - highest[None])
    return (
        highest,
        jnp.sum(scale * totals, axis=0),
        jnp.sum(expand(scale, output), axis=0),
    )


def heads_of(tensor):
    return tensor.reshape(tensor.shape[:-1] + (HEADS, HD))


def block_part(queries, keyside, values, allowed):
    head_size = queries.shape[-1]
    scores = jnp.einsum(
        "rqhe,rkhe->rqhk", queries, keyside, preferred_element_type=jnp.float32
    ) * head_size ** (-0.5)
    scores = jnp.where(allowed[:, :, None, :], scores, -jnp.inf)
    peaks = jnp.max(scores, axis=-1)
    weights = jnp.exp(scores - peaks[..., None]).astype(jnp.bfloat16)
    totals = jnp.sum(weights.astype(jnp.float32), axis=-1)
    output = jnp.einsum("rqhk,rkhe->rqhe", weights, values, preferred_element_type=jnp.float32)
    return (peaks, totals, output.reshape(output.shape[0], output.shape[1], -1))


def expand(factor, output):
    shaped = output.reshape(factor.shape + (-1,))
    return (shaped * factor[..., None]).reshape(output.shape)


def divide(output, totals):
    shaped = output.reshape(totals.shape + (-1,))
    return (shaped / totals[..., None]).reshape(output.shape)


def pair_join(former, latter):
    highest = jnp.maximum(former[0], latter[0])
    former_scale = jnp.exp(former[0] - highest)
    latter_scale = jnp.exp(latter[0] - highest)
    totals = former_scale * former[1] + latter_scale * latter[1]
    output = expand(former_scale, former[2]) + expand(latter_scale, latter[2])
    return (highest, totals, output)


def finish(joined):
    return divide(joined[2], joined[1]).astype(jnp.bfloat16)


def on_device(
    short_draft,
    short_mask,
    short_keys,
    short_values,
    short_length,
    short_x,
    accepted,
    long_draft,
    long_mask,
    long_keys,
    long_values,
    long_x,
    out_weight,
    norm_gain,
    router,
    route_ids,
    expert_in,
    expert_out,
):
    short_count = short_draft.shape[0]
    tree_size = short_draft.shape[1]
    cache_size = short_keys.shape[1]
    model_width = out_weight.shape[1]
    short_queries = heads_of(short_draft[:, :, 0])
    visible = jnp.broadcast_to(
        jnp.arange(cache_size)[None, None, :] < short_length[:, None, None],
        (short_count, tree_size, cache_size),
    )
    short_cache = block_part(short_queries, heads_of(short_keys), heads_of(short_values), visible)
    short_tree = block_part(
        short_queries,
        heads_of(short_draft[:, :, 1]),
        heads_of(short_draft[:, :, 2]),
        short_mask == 1,
    )
    short_attn = finish(pair_join(short_cache, short_tree))
    long_count = long_keys.shape[0]
    cache_local = long_keys.shape[1]
    long_queries = heads_of(long_draft[:, :, 0])
    everything = jnp.ones((long_count, tree_size, cache_local), dtype=bool)
    local_part = block_part(long_queries, heads_of(long_keys), heads_of(long_values), everything)
    share_rows = tree_size // lax.axis_size("blk")
    share_start = lax.axis_index("blk") * share_rows
    down_weight, projection = gather_blocks([expert_out[0]], out_weight, 0)
    cache_part = join_many(scatter_parts(local_part, share_rows))
    share_queries = lax.dynamic_slice_in_dim(long_queries, share_start, share_rows, 1)
    share_mask = lax.dynamic_slice_in_dim(long_mask, share_start, share_rows, 1)
    long_tree = block_part(
        share_queries, heads_of(long_draft[:, :, 1]), heads_of(long_draft[:, :, 2]), share_mask == 1
    )
    long_attn = finish(pair_join(cache_part, long_tree))
    attn_rows = jnp.concatenate(
        [short_attn.reshape(-1, short_attn.shape[-1]), long_attn.reshape(-1, long_attn.shape[-1])],
        axis=0,
    )
    residual = jnp.concatenate([short_x, long_x.reshape(-1, model_width)], axis=0)
    row_count = attn_rows.shape[0]
    projected = jnp.dot(
        attn_rows,
        projection,
        preferred_element_type=jnp.float32,
    )
    layer_state = (residual.astype(jnp.float32) + projected).astype(jnp.bfloat16)
    state_wide = layer_state.astype(jnp.float32)
    normed = (
        state_wide
        * lax.rsqrt(jnp.mean(state_wide * state_wide, axis=-1, keepdims=True) + 1e-06)
        * norm_gain.astype(jnp.float32)
    ).astype(jnp.bfloat16)
    gate_probs = jax.nn.sigmoid(jnp.dot(normed, router, preferred_element_type=jnp.float32))
    expert_count = router.shape[1]
    capacity = (row_count * 10 + 4 * expert_count - 1) // (4 * expert_count)
    one_hot = route_ids[:, :, None] == jnp.arange(expert_count, dtype=jnp.int32)[None, None, :]
    gate_pick = jnp.sum(jnp.where(one_hot, gate_probs[:, None, :], 0.0), axis=-1)
    flat_hot = one_hot.reshape(2 * row_count, expert_count).astype(jnp.int32)
    earlier = jnp.cumsum(flat_hot, axis=0) - flat_hot
    slot_in = jnp.sum(earlier * flat_hot, axis=-1)
    target = route_ids.reshape(-1) * capacity + slot_in
    placement = (
        jnp.arange(expert_count * capacity, dtype=jnp.int32)[:, None] == target[None, :]
    ).astype(jnp.bfloat16)
    dispatch = jnp.dot(
        placement, jnp.repeat(normed, 2, axis=0), preferred_element_type=jnp.float32
    ).astype(jnp.bfloat16)
    dispatch, own_in = lax.optimization_barrier((dispatch, expert_in))
    dispatch = dispatch.reshape(expert_count, capacity, model_width)
    received = lax.all_to_all(dispatch, "expert", split_axis=0, concat_axis=0, tiled=True)
    flat_rows = received.reshape(-1, model_width)
    gate_weight, up_weight = gather_blocks([own_in[0, :, 0, :], own_in[0, :, 1, :]], None, 1)
    gate_part = jnp.einsum("rd,nd->rn", flat_rows, gate_weight, preferred_element_type=jnp.float32)
    up_part = jnp.einsum("rd,nd->rn", flat_rows, up_weight, preferred_element_type=jnp.float32)
    inner_act = (jax.nn.gelu(gate_part, approximate=True) * up_part).astype(jnp.bfloat16)
    expert_sum = jnp.dot(inner_act, down_weight, preferred_element_type=jnp.float32)
    expert_y = expert_sum.astype(jnp.bfloat16).reshape(expert_count, capacity, model_width)
    returned = lax.all_to_all(expert_y, "expert", split_axis=0, concat_axis=0, tiled=True)
    per_route = jnp.einsum(
        "sa,sd->ad",
        placement,
        returned.reshape(-1, model_width),
        preferred_element_type=jnp.float32,
    )
    moe_sum = jnp.sum(per_route.reshape(row_count, 2, model_width) * gate_pick[:, :, None], axis=1)
    layer_out = (state_wide + moe_sum).astype(jnp.bfloat16)
    short_total = short_x.shape[0]
    short_out = layer_out[:short_total]
    long_out = layer_out[short_total:].reshape(long_x.shape)
    accepted_out = jnp.take_along_axis(
        short_out.reshape(short_count, tree_size, model_width), accepted[:, :, None], axis=1
    )
    return (short_out, accepted_out, long_out)


def solution(mesh):
    return jax.shard_map(
        on_device,
        mesh=mesh,
        in_specs=(
            P(("blk", "expert"), None, None, None),
            P(("blk", "expert"), None, None),
            P(("blk", "expert"), None, None),
            P(("blk", "expert"), None, None),
            P(("blk", "expert")),
            P(("blk", "expert"), None),
            P(("blk", "expert"), None),
            P("expert", None, None, None),
            P("expert", None, None),
            P("expert", "blk", None),
            P("expert", "blk", None),
            P("expert", "blk", None),
            P("expert", None),
            P(),
            P(),
            P(("blk", "expert"), None),
            P("expert", "blk", None, None),
            P("expert", "blk", None),
        ),
        out_specs=(
            P(("blk", "expert"), None),
            P(("blk", "expert"), None, None),
            P("expert", "blk", None),
        ),
        check_vma=False,
    )
```

```python
import functools
import jax
import jax.numpy as jnp
from jax import lax
from jax.experimental import pallas as pl
from jax.experimental.pallas import tpu as pltpu
from jax.sharding import PartitionSpec as P

HEADS = 8
HD = 64


LINE = 8
RING = 4
SLOT = 48


def sends_of(condition, descriptor, started):
    @pl.when(condition)
    def _():
        descriptor().start()

    started.append((condition, descriptor))


def remote(source, target, send_sem, recv_sem, device):
    return pltpu.make_async_remote_copy(
        src_ref=source,
        dst_ref=target,
        send_sem=send_sem,
        recv_sem=recv_sem,
        device_id=device,
        device_id_type=pl.DeviceIdType.MESH,
    )


def signal(barrier, device):
    pl.semaphore_signal(barrier, inc=1, device_id=device, device_id_type=pl.DeviceIdType.MESH)


def gather_kernel(count, with_rows, *refs):
    inputs = refs[:count]
    refs = refs[count:]
    if with_rows:
        rows_in, refs = refs[0], refs[1:]
    outputs = refs[:count]
    refs = refs[count:]
    if with_rows:
        rows_out, refs = refs[0], refs[1:]
    local_sem, recv_sem, up_sem, down_sem, right_sem, left_sem, far_sem = refs[:7]
    if with_rows:
        rows_local, rows_recv, rows_send = refs[7:]
    blk = lax.axis_index("blk")
    x = blk // LINE
    z = blk % LINE
    right = {"blk": ((x + 1) % RING) * LINE + z}
    left = {"blk": ((x + RING - 1) % RING) * LINE + z}
    above = {"blk": blk + 1}
    below = {"blk": blk - 1}
    has_up = z < LINE - 1
    has_down = z > 0
    started = []

    barrier = pltpu.get_barrier_semaphore()
    signal(barrier, right)
    signal(barrier, left)

    @pl.when(has_up)
    def _():
        signal(barrier, above)

    @pl.when(has_down)
    def _():
        signal(barrier, below)

    neighbours = 2 + has_up.astype(jnp.int32) + has_down.astype(jnp.int32)
    if with_rows:
        place = lax.axis_index("expert")
        half = place // 8
        y = (place // 2) % 4
        core = place % 2

        def at(h, row, c):
            return (h % 2) * 8 + (row % 4) * 2 + c % 2

        across = {"expert": at(half + 1, y, core)}
        partner = {"expert": at(half, y, core + 1)}
        ahead = {"expert": at(half, y + 1, core)}
        behind = {"expert": at(half, y + 3, core)}
        for device in (across, partner, ahead, behind):
            signal(barrier, device)
        neighbours = neighbours + 4
    pl.semaphore_wait(barrier, neighbours)

    def send(k, slot, source, sem, device):
        return lambda: remote(source(), outputs[k].at[slot], sem, recv_sem.at[k, slot], device)

    def arrive(k, slot):
        piece = outputs[k].at[slot]
        remote(piece, piece, far_sem.at[k, 0], recv_sem.at[k, slot], right).wait_recv()

    def row_send(index, slot, source, device):
        copy = remote(source, rows_out.at[slot], rows_send.at[index], rows_recv.at[slot], device)
        copy.start()
        row_started.append(copy)

    def row_arrive(slot):
        piece = rows_out.at[slot]
        remote(piece, piece, rows_send.at[0], rows_recv.at[slot], across).wait_recv()

    row_started = []
    always = z >= 0
    if with_rows:
        row_send(0, place, rows_in, across)
        own_rows = pltpu.make_async_copy(rows_in, rows_out.at[place], rows_local)
        own_rows.start()

    own_copies = []
    for k in range(count):
        own = lambda k=k: inputs[k]
        sends_of(has_up, send(k, blk, own, up_sem.at[k, 0], above), started)
        sends_of(has_down, send(k, blk, own, down_sem.at[k, 0], below), started)
        sends_of(always, send(k, blk, own, right_sem.at[k, 0], right), started)
        sends_of(always, send(k, blk, own, left_sem.at[k, 0], left), started)
        copy = pltpu.make_async_copy(inputs[k], outputs[k].at[blk], local_sem.at[k])
        copy.start()
        own_copies.append(copy)

    before = ((x + RING - 1) % RING) * LINE
    after = ((x + 1) % RING) * LINE
    opposite = ((x + 2) % RING) * LINE

    def pass_on(distance):
        for direction in (0, 1) if distance else (0,):
            line = z - distance if direction == 0 else z + distance
            present = z >= distance if direction == 0 else z + distance < LINE
            even = line % 2 == 0
            from_left, from_right = before + line, after + line
            for k in range(count):

                @pl.when(present)
                def _(k=k, from_left=from_left, from_right=from_right):
                    arrive(k, from_left)
                    arrive(k, from_right)

                sem = far_sem.at[k, distance + direction * LINE]
                first = lambda k=k, slot=from_left: outputs[k].at[slot]
                second = lambda k=k, slot=from_right: outputs[k].at[slot]
                sends_of(
                    jnp.logical_and(present, even),
                    send(k, from_left, first, sem, right),
                    started,
                )
                sends_of(
                    jnp.logical_and(present, jnp.logical_not(even)),
                    send(k, from_right, second, sem, left),
                    started,
                )

    for distance in range(1, LINE):
        for direction in (0, 1):
            slot = blk - distance if direction == 0 else blk + distance
            present = z >= distance if direction == 0 else z + distance < LINE
            onward = has_up if direction == 0 else has_down
            target = above if direction == 0 else below
            z_sem = up_sem if direction == 0 else down_sem
            index = distance + direction * LINE
            for k in range(count):
                held = lambda k=k, slot=slot: outputs[k].at[slot]

                @pl.when(present)
                def _(k=k, slot=slot):
                    arrive(k, slot)

                sends_of(
                    jnp.logical_and(present, onward),
                    send(k, slot, held, z_sem.at[k, distance], target),
                    started,
                )
                sends_of(present, send(k, slot, held, right_sem.at[k, index], right), started)
                sends_of(present, send(k, slot, held, left_sem.at[k, index], left), started)
        if distance in (2, 4, 6):
            pass_on(distance // 2 - 1)
        if with_rows and distance == 2:
            row_arrive(at(half + 1, y, core))
            for h in range(2):
                slot = at(half + h, y, core)
                source = rows_in if h == 0 else rows_out.at[slot]
                row_send(1 + h, slot, source, partner)
        if with_rows and distance == 3:
            for h in range(2):
                row_arrive(at(half + h, y, core + 1))
            for h in range(2):
                for c in range(2):
                    slot = at(half + h, y, core + c)
                    source = rows_in if h + c == 0 else rows_out.at[slot]
                    row_send(3 + 2 * h + c, slot, source, ahead)
                    row_send(7 + 2 * h + c, slot, source, behind)
        if with_rows and distance == 6:
            for c in range(2):
                for h in range(2):
                    row_arrive(at(h, y + 3, c))
                    row_arrive(at(h, y + 1, c))
                slot = at(0, y + 3, c)
                row_send(11 + c, slot, rows_out.at[slot], ahead)
                slot = at(1, y + 1, c)
                row_send(13 + c, slot, rows_out.at[slot], behind)

    for distance in range(3, LINE):
        pass_on(distance)
    for line in range(LINE):
        for k in range(count):
            arrive(k, opposite + line)
    if with_rows:
        for h in range(2):
            for c in range(2):
                row_arrive(at(h, y + 2, c))
        for copy in row_started:
            copy.wait_send()
        own_rows.wait()
    for copy in own_copies:
        copy.wait()
    for condition, descriptor in started:

        @pl.when(condition)
        def _(descriptor=descriptor):
            descriptor().wait_send()


def gather_blocks(blocks, rows, collective_id):
    count = len(blocks)
    with_rows = rows is not None
    blocks = [jnp.pad(block, ((0, SLOT - block.shape[0]), (0, 0))) for block in blocks]
    width = blocks[0].shape[1]
    dma = pltpu.SemaphoreType.DMA
    shapes = [jax.ShapeDtypeStruct((RING * LINE, SLOT, width), jnp.bfloat16)] * count
    operands = list(blocks)
    scratch = [
        dma((count,)),
        dma((count, RING * LINE)),
        dma((count, LINE)),
        dma((count, LINE)),
        dma((count, 2 * LINE)),
        dma((count, 2 * LINE)),
        dma((count, 2 * LINE)),
    ]
    if with_rows:
        operands.append(rows)
        shapes.append(jax.ShapeDtypeStruct((16,) + rows.shape, jnp.bfloat16))
        scratch += [dma(()), dma((16,)), dma((15,))]
    gathered = pl.pallas_call(
        functools.partial(gather_kernel, count, with_rows),
        out_shape=shapes,
        in_specs=[pl.BlockSpec(memory_space=pltpu.VMEM)] * len(operands),
        out_specs=[pl.BlockSpec(memory_space=pl.ANY)] * len(shapes),
        scratch_shapes=scratch,
        compiler_params=pltpu.CompilerParams(collective_id=collective_id, has_side_effects=True),
        cost_estimate=pl.CostEstimate(
            flops=0, bytes_accessed=100_000_000 * count, transcendentals=0
        ),
    )(*operands)
    return [array.reshape(-1, array.shape[-1]) for array in gathered]


def scatter_parts(part, share_rows):
    peaks, totals, output = part
    count, tree = peaks.shape[:2]
    packed = jnp.concatenate([output, peaks, totals], axis=-1)
    width = packed.shape[-1]
    packed = packed.reshape(count, tree // share_rows, share_rows, width).transpose(1, 0, 2, 3)
    arrived = lax.all_to_all(packed, "blk", split_axis=0, concat_axis=0, tiled=True)
    wide = output.shape[-1]
    return (
        arrived[..., wide : wide + HEADS],
        arrived[..., wide + HEADS :],
        arrived[..., :wide],
    )


def join_many(parts):
    peaks, totals, output = parts
    highest = jnp.max(peaks, axis=0)
    scale = jnp.exp(peaks - highest[None])
    return (
        highest,
        jnp.sum(scale * totals, axis=0),
        jnp.sum(expand(scale, output), axis=0),
    )


def heads_of(tensor):
    return tensor.reshape(tensor.shape[:-1] + (HEADS, HD))


def block_part(queries, keyside, values, allowed):
    head_size = queries.shape[-1]
    scores = jnp.einsum(
        "rqhe,rkhe->rqhk", queries, keyside, preferred_element_type=jnp.float32
    ) * head_size ** (-0.5)
    scores = jnp.where(allowed[:, :, None, :], scores, -jnp.inf)
    peaks = jnp.max(scores, axis=-1)
    weights = jnp.exp(scores - peaks[..., None]).astype(jnp.bfloat16)
    totals = jnp.sum(weights.astype(jnp.float32), axis=-1)
    output = jnp.einsum("rqhk,rkhe->rqhe", weights, values, preferred_element_type=jnp.float32)
    return (peaks, totals, output.reshape(output.shape[0], output.shape[1], -1))


def expand(factor, output):
    shaped = output.reshape(factor.shape + (-1,))
    return (shaped * factor[..., None]).reshape(output.shape)


def divide(output, totals):
    shaped = output.reshape(totals.shape + (-1,))
    return (shaped / totals[..., None]).reshape(output.shape)


def pair_join(former, latter):
    highest = jnp.maximum(former[0], latter[0])
    former_scale = jnp.exp(former[0] - highest)
    latter_scale = jnp.exp(latter[0] - highest)
    totals = former_scale * former[1] + latter_scale * latter[1]
    output = expand(former_scale, former[2]) + expand(latter_scale, latter[2])
    return (highest, totals, output)


def finish(joined):
    return divide(joined[2], joined[1]).astype(jnp.bfloat16)


def on_device(
    short_draft,
    short_mask,
    short_keys,
    short_values,
    short_length,
    short_x,
    accepted,
    long_draft,
    long_mask,
    long_keys,
    long_values,
    long_x,
    out_weight,
    norm_gain,
    router,
    route_ids,
    expert_in,
    expert_out,
):
    short_count = short_draft.shape[0]
    tree_size = short_draft.shape[1]
    cache_size = short_keys.shape[1]
    model_width = out_weight.shape[1]
    short_queries = heads_of(short_draft[:, :, 0])
    visible = jnp.broadcast_to(
        jnp.arange(cache_size)[None, None, :] < short_length[:, None, None],
        (short_count, tree_size, cache_size),
    )
    short_cache = block_part(short_queries, heads_of(short_keys), heads_of(short_values), visible)
    short_tree = block_part(
        short_queries,
        heads_of(short_draft[:, :, 1]),
        heads_of(short_draft[:, :, 2]),
        short_mask == 1,
    )
    short_attn = finish(pair_join(short_cache, short_tree))
    long_count = long_keys.shape[0]
    cache_local = long_keys.shape[1]
    long_queries = heads_of(long_draft[:, :, 0])
    everything = jnp.ones((long_count, tree_size, cache_local), dtype=bool)
    local_part = block_part(long_queries, heads_of(long_keys), heads_of(long_values), everything)
    share_rows = tree_size // lax.axis_size("blk")
    share_start = lax.axis_index("blk") * share_rows
    down_weight, projection = gather_blocks([expert_out[0]], out_weight, 0)
    cache_part = join_many(scatter_parts(local_part, share_rows))
    share_queries = lax.dynamic_slice_in_dim(long_queries, share_start, share_rows, 1)
    share_mask = lax.dynamic_slice_in_dim(long_mask, share_start, share_rows, 1)
    long_tree = block_part(
        share_queries, heads_of(long_draft[:, :, 1]), heads_of(long_draft[:, :, 2]), share_mask == 1
    )
    long_attn = finish(pair_join(cache_part, long_tree))
    attn_rows = jnp.concatenate(
        [short_attn.reshape(-1, short_attn.shape[-1]), long_attn.reshape(-1, long_attn.shape[-1])],
        axis=0,
    )
    residual = jnp.concatenate([short_x, long_x.reshape(-1, model_width)], axis=0)
    row_count = attn_rows.shape[0]
    projected = jnp.dot(
        attn_rows,
        projection,
        preferred_element_type=jnp.float32,
    )
    layer_state = (residual.astype(jnp.float32) + projected).astype(jnp.bfloat16)
    state_wide = layer_state.astype(jnp.float32)
    normed = (
        state_wide
        * lax.rsqrt(jnp.mean(state_wide * state_wide, axis=-1, keepdims=True) + 1e-06)
        * norm_gain.astype(jnp.float32)
    ).astype(jnp.bfloat16)
    gate_probs = jax.nn.sigmoid(jnp.dot(normed, router, preferred_element_type=jnp.float32))
    expert_count = router.shape[1]
    capacity = (row_count * 10 + 4 * expert_count - 1) // (4 * expert_count)
    one_hot = route_ids[:, :, None] == jnp.arange(expert_count, dtype=jnp.int32)[None, None, :]
    gate_pick = jnp.sum(jnp.where(one_hot, gate_probs[:, None, :], 0.0), axis=-1)
    flat_hot = one_hot.reshape(2 * row_count, expert_count).astype(jnp.int32)
    earlier = jnp.cumsum(flat_hot, axis=0) - flat_hot
    slot_in = jnp.sum(earlier * flat_hot, axis=-1)
    target = route_ids.reshape(-1) * capacity + slot_in
    placement = (
        jnp.arange(expert_count * capacity, dtype=jnp.int32)[:, None] == target[None, :]
    ).astype(jnp.bfloat16)
    dispatch = jnp.dot(
        placement, jnp.repeat(normed, 2, axis=0), preferred_element_type=jnp.float32
    ).astype(jnp.bfloat16)
    dispatch, own_in = lax.optimization_barrier((dispatch, expert_in))
    dispatch = dispatch.reshape(expert_count, capacity, model_width)
    received = lax.all_to_all(dispatch, "expert", split_axis=0, concat_axis=0, tiled=True)
    flat_rows = received.reshape(-1, model_width)
    gate_weight, up_weight = gather_blocks([own_in[0, :, 0, :], own_in[0, :, 1, :]], None, 1)
    gate_part = jnp.einsum("rd,nd->rn", flat_rows, gate_weight, preferred_element_type=jnp.float32)
    up_part = jnp.einsum("rd,nd->rn", flat_rows, up_weight, preferred_element_type=jnp.float32)
    inner_act = (jax.nn.gelu(gate_part, approximate=True) * up_part).astype(jnp.bfloat16)
    expert_sum = jnp.dot(inner_act, down_weight, preferred_element_type=jnp.float32)
    expert_y = expert_sum.astype(jnp.bfloat16).reshape(expert_count, capacity, model_width)
    returned = lax.all_to_all(expert_y, "expert", split_axis=0, concat_axis=0, tiled=True)
    per_route = jnp.einsum(
        "sa,sd->ad",
        placement,
        returned.reshape(-1, model_width),
        preferred_element_type=jnp.float32,
    )
    moe_sum = jnp.sum(per_route.reshape(row_count, 2, model_width) * gate_pick[:, :, None], axis=1)
    layer_out = (state_wide + moe_sum).astype(jnp.bfloat16)
    short_total = short_x.shape[0]
    short_out = layer_out[:short_total]
    long_out = layer_out[short_total:].reshape(long_x.shape)
    accepted_out = jnp.take_along_axis(
        short_out.reshape(short_count, tree_size, model_width), accepted[:, :, None], axis=1
    )
    return (short_out, accepted_out, long_out)


def solution(mesh):
    return jax.shard_map(
        on_device,
        mesh=mesh,
        in_specs=(
            P(("blk", "expert"), None, None, None),
            P(("blk", "expert"), None, None),
            P(("blk", "expert"), None, None),
            P(("blk", "expert"), None, None),
            P(("blk", "expert")),
            P(("blk", "expert"), None),
            P(("blk", "expert"), None),
            P("expert", None, None, None),
            P("expert", None, None),
            P("expert", "blk", None),
            P("expert", "blk", None),
            P("expert", "blk", None),
            P("expert", None),
            P(),
            P(),
            P(("blk", "expert"), None),
            P("expert", "blk", None, None),
            P("expert", "blk", None),
        ),
        out_specs=(
            P(("blk", "expert"), None),
            P(("blk", "expert"), None, None),
            P("expert", "blk", None),
        ),
        check_vma=False,
    )
```

```python
import functools
import jax
import jax.numpy as jnp
from jax import lax
from jax.experimental import pallas as pl
from jax.experimental.pallas import tpu as pltpu
from jax.sharding import PartitionSpec as P

HEADS = 8
HD = 64


LINE = 8
RING = 4
SLOT = 48


def sends_of(condition, descriptor, started):
    @pl.when(condition)
    def _():
        descriptor().start()

    started.append((condition, descriptor))


def remote(source, target, send_sem, recv_sem, device):
    return pltpu.make_async_remote_copy(
        src_ref=source,
        dst_ref=target,
        send_sem=send_sem,
        recv_sem=recv_sem,
        device_id=device,
        device_id_type=pl.DeviceIdType.MESH,
    )


def signal(barrier, device):
    pl.semaphore_signal(barrier, inc=1, device_id=device, device_id_type=pl.DeviceIdType.MESH)


def gather_kernel(count, with_rows, *refs):
    inputs = refs[:count]
    refs = refs[count:]
    if with_rows:
        rows_in, refs = refs[0], refs[1:]
    outputs = refs[:count]
    refs = refs[count:]
    if with_rows:
        rows_out, refs = refs[0], refs[1:]
    local_sem, recv_sem, up_sem, down_sem, right_sem, left_sem, far_sem = refs[:7]
    if with_rows:
        rows_local, rows_recv, rows_send = refs[7:]
    blk = lax.axis_index("blk")
    x = blk // LINE
    z = blk % LINE
    right = {"blk": ((x + 1) % RING) * LINE + z}
    left = {"blk": ((x + RING - 1) % RING) * LINE + z}
    above = {"blk": blk + 1}
    below = {"blk": blk - 1}
    has_up = z < LINE - 1
    has_down = z > 0
    started = []

    barrier = pltpu.get_barrier_semaphore()
    signal(barrier, right)
    signal(barrier, left)

    @pl.when(has_up)
    def _():
        signal(barrier, above)

    @pl.when(has_down)
    def _():
        signal(barrier, below)

    neighbours = 2 + has_up.astype(jnp.int32) + has_down.astype(jnp.int32)
    if with_rows:
        place = lax.axis_index("expert")
        half = place // 8
        y = (place // 2) % 4
        core = place % 2

        def at(h, row, c):
            return (h % 2) * 8 + (row % 4) * 2 + c % 2

        across = {"expert": at(half + 1, y, core)}
        partner = {"expert": at(half, y, core + 1)}
        ahead = {"expert": at(half, y + 1, core)}
        behind = {"expert": at(half, y + 3, core)}
        for device in (across, partner, ahead, behind):
            signal(barrier, device)
        neighbours = neighbours + 4
    pl.semaphore_wait(barrier, neighbours)

    def send(k, slot, source, sem, device):
        return lambda: remote(source(), outputs[k].at[:, slot], sem, recv_sem.at[k, slot], device)

    def arrive(k, slot):
        piece = outputs[k].at[:, slot]
        remote(piece, piece, far_sem.at[k, 0], recv_sem.at[k, slot], right).wait_recv()

    def row_send(index, slot, source, device):
        copy = remote(source, rows_out.at[slot], rows_send.at[index], rows_recv.at[slot], device)
        copy.start()
        row_started.append(copy)

    def row_arrive(slot):
        piece = rows_out.at[slot]
        remote(piece, piece, rows_send.at[0], rows_recv.at[slot], across).wait_recv()

    row_started = []
    always = z >= 0
    if with_rows:
        row_send(0, place, rows_in, across)
        own_rows = pltpu.make_async_copy(rows_in, rows_out.at[place], rows_local)
        own_rows.start()

    own_copies = []
    for k in range(count):
        own = lambda k=k: inputs[k]
        sends_of(has_up, send(k, blk, own, up_sem.at[k, 0], above), started)
        sends_of(has_down, send(k, blk, own, down_sem.at[k, 0], below), started)
        sends_of(always, send(k, blk, own, right_sem.at[k, 0], right), started)
        sends_of(always, send(k, blk, own, left_sem.at[k, 0], left), started)
        copy = pltpu.make_async_copy(inputs[k], outputs[k].at[:, blk], local_sem.at[k])
        copy.start()
        own_copies.append(copy)

    before = ((x + RING - 1) % RING) * LINE
    after = ((x + 1) % RING) * LINE
    opposite = ((x + 2) % RING) * LINE

    def pass_on(distance):
        for direction in (0, 1) if distance else (0,):
            line = z - distance if direction == 0 else z + distance
            present = z >= distance if direction == 0 else z + distance < LINE
            even = line % 2 == 0
            from_left, from_right = before + line, after + line
            for k in range(count):

                @pl.when(present)
                def _(k=k, from_left=from_left, from_right=from_right):
                    arrive(k, from_left)
                    arrive(k, from_right)

                sem = far_sem.at[k, distance + direction * LINE]
                first = lambda k=k, slot=from_left: outputs[k].at[:, slot]
                second = lambda k=k, slot=from_right: outputs[k].at[:, slot]
                sends_of(
                    jnp.logical_and(present, even),
                    send(k, from_left, first, sem, right),
                    started,
                )
                sends_of(
                    jnp.logical_and(present, jnp.logical_not(even)),
                    send(k, from_right, second, sem, left),
                    started,
                )

    for distance in range(1, LINE):
        for direction in (0, 1):
            slot = blk - distance if direction == 0 else blk + distance
            present = z >= distance if direction == 0 else z + distance < LINE
            onward = has_up if direction == 0 else has_down
            target = above if direction == 0 else below
            z_sem = up_sem if direction == 0 else down_sem
            index = distance + direction * LINE
            for k in range(count):
                held = lambda k=k, slot=slot: outputs[k].at[:, slot]

                @pl.when(present)
                def _(k=k, slot=slot):
                    arrive(k, slot)

                sends_of(
                    jnp.logical_and(present, onward),
                    send(k, slot, held, z_sem.at[k, distance], target),
                    started,
                )
                sends_of(present, send(k, slot, held, right_sem.at[k, index], right), started)
                sends_of(present, send(k, slot, held, left_sem.at[k, index], left), started)
        if distance in (2, 4, 6):
            pass_on(distance // 2 - 1)
        if with_rows and distance == 2:
            row_arrive(at(half + 1, y, core))
            for h in range(2):
                slot = at(half + h, y, core)
                source = rows_in if h == 0 else rows_out.at[slot]
                row_send(1 + h, slot, source, partner)
        if with_rows and distance == 3:
            for h in range(2):
                row_arrive(at(half + h, y, core + 1))
            for h in range(2):
                for c in range(2):
                    slot = at(half + h, y, core + c)
                    source = rows_in if h + c == 0 else rows_out.at[slot]
                    row_send(3 + 2 * h + c, slot, source, ahead)
                    row_send(7 + 2 * h + c, slot, source, behind)
        if with_rows and distance == 6:
            for c in range(2):
                for h in range(2):
                    row_arrive(at(h, y + 3, c))
                    row_arrive(at(h, y + 1, c))
                slot = at(0, y + 3, c)
                row_send(11 + c, slot, rows_out.at[slot], ahead)
                slot = at(1, y + 1, c)
                row_send(13 + c, slot, rows_out.at[slot], behind)

    for distance in range(3, LINE):
        pass_on(distance)
    for line in range(LINE):
        for k in range(count):
            arrive(k, opposite + line)
    if with_rows:
        for h in range(2):
            for c in range(2):
                row_arrive(at(h, y + 2, c))
        for copy in row_started:
            copy.wait_send()
        own_rows.wait()
    for copy in own_copies:
        copy.wait()
    for condition, descriptor in started:

        @pl.when(condition)
        def _(descriptor=descriptor):
            descriptor().wait_send()


def gather_blocks(blocks, rows, collective_id):
    count = len(blocks)
    with_rows = rows is not None
    blocks = [jnp.pad(block, ((0, 0), (0, SLOT - block.shape[1]), (0, 0))) for block in blocks]
    layers, _, width = blocks[0].shape
    dma = pltpu.SemaphoreType.DMA
    shapes = [jax.ShapeDtypeStruct((layers, RING * LINE, SLOT, width), jnp.bfloat16)] * count
    operands = list(blocks)
    scratch = [
        dma((count,)),
        dma((count, RING * LINE)),
        dma((count, LINE)),
        dma((count, LINE)),
        dma((count, 2 * LINE)),
        dma((count, 2 * LINE)),
        dma((count, 2 * LINE)),
    ]
    if with_rows:
        operands.append(rows)
        shapes.append(jax.ShapeDtypeStruct((16,) + rows.shape, jnp.bfloat16))
        scratch += [dma(()), dma((16,)), dma((15,))]
    gathered = pl.pallas_call(
        functools.partial(gather_kernel, count, with_rows),
        out_shape=shapes,
        in_specs=[pl.BlockSpec(memory_space=pltpu.VMEM)] * len(operands),
        out_specs=[pl.BlockSpec(memory_space=pl.ANY)] * len(shapes),
        scratch_shapes=scratch,
        compiler_params=pltpu.CompilerParams(collective_id=collective_id, has_side_effects=True),
        cost_estimate=pl.CostEstimate(
            flops=0, bytes_accessed=100_000_000 * layers, transcendentals=0
        ),
    )(*operands)
    weights = gathered[0].reshape(layers, -1, width)
    if with_rows:
        return weights, gathered[1].reshape(-1, rows.shape[-1])
    return weights


def scatter_parts(part, share_rows):
    peaks, totals, output = part
    count, tree = peaks.shape[:2]
    packed = jnp.concatenate([output, peaks, totals], axis=-1)
    width = packed.shape[-1]
    packed = packed.reshape(count, tree // share_rows, share_rows, width).transpose(1, 0, 2, 3)
    arrived = lax.all_to_all(packed, "blk", split_axis=0, concat_axis=0, tiled=True)
    wide = output.shape[-1]
    return (
        arrived[..., wide : wide + HEADS],
        arrived[..., wide + HEADS :],
        arrived[..., :wide],
    )


def join_many(parts):
    peaks, totals, output = parts
    highest = jnp.max(peaks, axis=0)
    scale = jnp.exp(peaks - highest[None])
    return (
        highest,
        jnp.sum(scale * totals, axis=0),
        jnp.sum(expand(scale, output), axis=0),
    )


def heads_of(tensor):
    return tensor.reshape(tensor.shape[:-1] + (HEADS, HD))


def block_part(queries, keyside, values, allowed):
    head_size = queries.shape[-1]
    scores = jnp.einsum(
        "rqhe,rkhe->rqhk", queries, keyside, preferred_element_type=jnp.float32
    ) * head_size ** (-0.5)
    scores = jnp.where(allowed[:, :, None, :], scores, -jnp.inf)
    peaks = jnp.max(scores, axis=-1)
    weights = jnp.exp(scores - peaks[..., None]).astype(jnp.bfloat16)
    totals = jnp.sum(weights.astype(jnp.float32), axis=-1)
    output = jnp.einsum("rqhk,rkhe->rqhe", weights, values, preferred_element_type=jnp.float32)
    return (peaks, totals, output.reshape(output.shape[0], output.shape[1], -1))


def expand(factor, output):
    shaped = output.reshape(factor.shape + (-1,))
    return (shaped * factor[..., None]).reshape(output.shape)


def divide(output, totals):
    shaped = output.reshape(totals.shape + (-1,))
    return (shaped / totals[..., None]).reshape(output.shape)


def pair_join(former, latter):
    highest = jnp.maximum(former[0], latter[0])
    former_scale = jnp.exp(former[0] - highest)
    latter_scale = jnp.exp(latter[0] - highest)
    totals = former_scale * former[1] + latter_scale * latter[1]
    output = expand(former_scale, former[2]) + expand(latter_scale, latter[2])
    return (highest, totals, output)


def finish(joined):
    return divide(joined[2], joined[1]).astype(jnp.bfloat16)


def on_device(
    short_draft,
    short_mask,
    short_keys,
    short_values,
    short_length,
    short_x,
    accepted,
    long_draft,
    long_mask,
    long_keys,
    long_values,
    long_x,
    out_weight,
    norm_gain,
    router,
    route_ids,
    expert_in,
    expert_out,
):
    short_count = short_draft.shape[0]
    tree_size = short_draft.shape[1]
    cache_size = short_keys.shape[1]
    model_width = out_weight.shape[1]
    short_queries = heads_of(short_draft[:, :, 0])
    visible = jnp.broadcast_to(
        jnp.arange(cache_size)[None, None, :] < short_length[:, None, None],
        (short_count, tree_size, cache_size),
    )
    short_cache = block_part(short_queries, heads_of(short_keys), heads_of(short_values), visible)
    short_tree = block_part(
        short_queries,
        heads_of(short_draft[:, :, 1]),
        heads_of(short_draft[:, :, 2]),
        short_mask == 1,
    )
    short_attn = finish(pair_join(short_cache, short_tree))
    long_count = long_keys.shape[0]
    cache_local = long_keys.shape[1]
    long_queries = heads_of(long_draft[:, :, 0])
    everything = jnp.ones((long_count, tree_size, cache_local), dtype=bool)
    local_part = block_part(long_queries, heads_of(long_keys), heads_of(long_values), everything)
    share_rows = tree_size // lax.axis_size("blk")
    share_start = lax.axis_index("blk") * share_rows
    down_weight, projection = gather_blocks([expert_out], out_weight, 0)
    cache_part = join_many(scatter_parts(local_part, share_rows))
    share_queries = lax.dynamic_slice_in_dim(long_queries, share_start, share_rows, 1)
    share_mask = lax.dynamic_slice_in_dim(long_mask, share_start, share_rows, 1)
    long_tree = block_part(
        share_queries, heads_of(long_draft[:, :, 1]), heads_of(long_draft[:, :, 2]), share_mask == 1
    )
    long_attn = finish(pair_join(cache_part, long_tree))
    attn_rows = jnp.concatenate(
        [short_attn.reshape(-1, short_attn.shape[-1]), long_attn.reshape(-1, long_attn.shape[-1])],
        axis=0,
    )
    residual = jnp.concatenate([short_x, long_x.reshape(-1, model_width)], axis=0)
    row_count = attn_rows.shape[0]
    projected = jnp.dot(
        attn_rows,
        projection,
        preferred_element_type=jnp.float32,
    )
    layer_state = (residual.astype(jnp.float32) + projected).astype(jnp.bfloat16)
    state_wide = layer_state.astype(jnp.float32)
    normed = (
        state_wide
        * lax.rsqrt(jnp.mean(state_wide * state_wide, axis=-1, keepdims=True) + 1e-06)
        * norm_gain.astype(jnp.float32)
    ).astype(jnp.bfloat16)
    gate_probs = jax.nn.sigmoid(jnp.dot(normed, router, preferred_element_type=jnp.float32))
    expert_count = router.shape[1]
    capacity = (row_count * 10 + 4 * expert_count - 1) // (4 * expert_count)
    one_hot = route_ids[:, :, None] == jnp.arange(expert_count, dtype=jnp.int32)[None, None, :]
    gate_pick = jnp.sum(jnp.where(one_hot, gate_probs[:, None, :], 0.0), axis=-1)
    flat_hot = one_hot.reshape(2 * row_count, expert_count).astype(jnp.int32)
    earlier = jnp.cumsum(flat_hot, axis=0) - flat_hot
    slot_in = jnp.sum(earlier * flat_hot, axis=-1)
    target = route_ids.reshape(-1) * capacity + slot_in
    placement = (
        jnp.arange(expert_count * capacity, dtype=jnp.int32)[:, None] == target[None, :]
    ).astype(jnp.bfloat16)
    dispatch = jnp.dot(
        placement, jnp.repeat(normed, 2, axis=0), preferred_element_type=jnp.float32
    ).astype(jnp.bfloat16)
    dispatch, own_in = lax.optimization_barrier((dispatch, expert_in))
    dispatch = dispatch.reshape(expert_count, capacity, model_width)
    received = lax.all_to_all(dispatch, "expert", split_axis=0, concat_axis=0, tiled=True)
    flat_rows = received.reshape(-1, model_width)
    gate_weight, up_weight = gather_blocks([own_in[0].transpose(1, 0, 2)], None, 1)
    gate_part = jnp.einsum("rd,nd->rn", flat_rows, gate_weight, preferred_element_type=jnp.float32)
    up_part = jnp.einsum("rd,nd->rn", flat_rows, up_weight, preferred_element_type=jnp.float32)
    inner_act = (jax.nn.gelu(gate_part, approximate=True) * up_part).astype(jnp.bfloat16)
    expert_sum = jnp.dot(inner_act, down_weight[0], preferred_element_type=jnp.float32)
    expert_y = expert_sum.astype(jnp.bfloat16).reshape(expert_count, capacity, model_width)
    returned = lax.all_to_all(expert_y, "expert", split_axis=0, concat_axis=0, tiled=True)
    per_route = jnp.einsum(
        "sa,sd->ad",
        placement,
        returned.reshape(-1, model_width),
        preferred_element_type=jnp.float32,
    )
    moe_sum = jnp.sum(per_route.reshape(row_count, 2, model_width) * gate_pick[:, :, None], axis=1)
    layer_out = (state_wide + moe_sum).astype(jnp.bfloat16)
    short_total = short_x.shape[0]
    short_out = layer_out[:short_total]
    long_out = layer_out[short_total:].reshape(long_x.shape)
    accepted_out = jnp.take_along_axis(
        short_out.reshape(short_count, tree_size, model_width), accepted[:, :, None], axis=1
    )
    return (short_out, accepted_out, long_out)


def solution(mesh):
    return jax.shard_map(
        on_device,
        mesh=mesh,
        in_specs=(
            P(("blk", "expert"), None, None, None),
            P(("blk", "expert"), None, None),
            P(("blk", "expert"), None, None),
            P(("blk", "expert"), None, None),
            P(("blk", "expert")),
            P(("blk", "expert"), None),
            P(("blk", "expert"), None),
            P("expert", None, None, None),
            P("expert", None, None),
            P("expert", "blk", None),
            P("expert", "blk", None),
            P("expert", "blk", None),
            P("expert", None),
            P(),
            P(),
            P(("blk", "expert"), None),
            P("expert", "blk", None, None),
            P("expert", "blk", None),
        ),
        out_specs=(
            P(("blk", "expert"), None),
            P(("blk", "expert"), None, None),
            P("expert", "blk", None),
        ),
        check_vma=False,
    )
```
